32 devices in a mesh: scen: 8 (over z, core), dec: 4 (over y, x).
Axes of the slice: x: 2, y: 2, z: 4, core: 2. Of those that a mesh axis runs over, the one named last changes fastest.
Arguments:
- order_qty: bfloat16 [8192, 4096], P('dec', 'scen'), may hold values from 0 to 2
- multiplier: float32 [8192, 4096], P('dec', 'scen'), may hold values from -6 to 6
- unit_cost: bfloat16 [8192, 4096], P('dec', 'scen'), may hold values from -6 to 6
- demand: bfloat16 [2048, 4096], P('dec', 'scen'), may hold values from -6 to 6
- technology: bfloat16 [8192, 2048], P('dec'), may hold values from -0.0625 to 0.0625
- kkt_inverse: bfloat16 [2048, 2048], P('dec'), may hold values from -1 to 3
- probability: float32 [4096], P('scen'), may hold values from 0.1 to 1
- scenario_node: int32 [4096, 1], P('scen'), may hold values from 0 to 511
Outputs:
- planned: bfloat16 [8192, 4096], P('dec', 'scen')
- recourse: bfloat16 [2048, 4096], P('dec', 'scen')
- consensus: float32 [8192, 512], P('dec')
- multiplier_next: float32 [8192, 4096], P('dec', 'scen')
The draws below stay inside these ranges and needn't reach their ends.
Inputs may be any that keep to these rules, and one draw needn't show every extreme that they name: `scenario_node`: every one of the 512 nodes is the node of some scenario.
All inputs are finite; a program needn't handle non-finite values.
Results may differ from the reference program's by a relative error of at most 0.023.
Values may be sent and summed in bfloat16 or wider, within the bound.
No kernel may reach another device: no remote copies, remote signals or barrier semaphores. Data moves between devices by JAX's collectives and lax.ppermute only.
A program may use at most 128 MiB of HBM per device.

```python
import math
import jax
import jax.numpy as jnp
from jax import lax

NX = 8192
M = 2048
G = 512
SCEN = 4096


def draw_kkt_inverse(key, part):
    first, second = jax.random.split(key)
    base = jnp.clip(jax.random.normal(first, (M, M), jnp.float32), -4.0, 4.0)
    offdiag = (base + base.T) * (0.5 / jnp.sqrt(jnp.float32(M)))
    diagonal = jax.random.uniform(second, (M,), jnp.float32, 1.0, 2.0)
    return (offdiag + jnp.diag(diagonal)).astype(jnp.bfloat16)


def steps_of(rng, dims, pieces, low, top_value):
    loudness = 1.0
    for axis_at, blocks in pieces:
        heights = jax.random.uniform(jax.random.fold_in(jax.random.fold_in(rng, 6), axis_at), (blocks,), jnp.float32, low / len(pieces), top_value / len(pieces))
        loudness = loudness * jnp.repeat(jnp.exp(heights), dims[axis_at] // blocks).reshape((-1,) + (1,) * (len(dims) - 1 - axis_at))
    return loudness


def different_ones(rng, rows, count, top, lift):
    order = jax.random.permutation(jax.random.fold_in(rng, 1), count)
    favour = order
    for power in range(3):
        favour = favour * favour // count
    favour = favour * lift // count
    chance = jax.random.randint(jax.random.fold_in(rng, 2), (rows, count), 0, 4096) + favour
    sure = jax.random.permutation(jax.random.fold_in(rng, 3), rows)[jnp.arange(count) % rows]
    chance = jnp.where(jnp.arange(rows)[:, None] == sure[None, :], 1 << 14, chance)
    merit = chance * count + jnp.arange(count)
    return lax.top_k(merit.astype(jnp.int32), top)[1].astype(jnp.int32)


def scatter_about(stream_key, extent, spread, most, shards=(), kind=jnp.bfloat16):
    array = spread * jax.random.normal(stream_key, extent, jnp.float32)
    if shards:
        array = array * steps_of(stream_key, extent, shards, -0.22, 0.18)
    return jnp.clip(array, -most, most).astype(kind)


def setup_inputs(seed: int = 0) -> dict:
    arg_keys = jax.random.split(jax.random.key(seed), 9)
    order_qty = jnp.clip(2.0 * jax.random.uniform(arg_keys[0], (NX, SCEN), jnp.float32) ** steps_of(arg_keys[0], (NX, SCEN), ((0, 4), (1, 8)), -0.2, 0.2), 0.0, 2.0).astype(jnp.bfloat16)
    multiplier = scatter_about(arg_keys[1], (NX, SCEN), 1.0, 6.0, ((0, 4), (1, 8)), jnp.float32)
    unit_cost = scatter_about(arg_keys[2], (NX, SCEN), 1.0, 6.0, ((0, 4), (1, 8)))
    demand = scatter_about(arg_keys[3], (M, SCEN), 1.0, 6.0, ((0, 4), (1, 8)))
    technology = scatter_about(arg_keys[4], (NX, M), NX ** -0.5, 0.0625, ((0, 4),))
    kkt_inverse = draw_kkt_inverse(jax.random.fold_in(arg_keys[8], 71), 0)
    probability = jnp.clip(jnp.exp(math.log(1.0) - 2.3025851 * jax.random.uniform(arg_keys[6], (SCEN,), jnp.float32) ** steps_of(arg_keys[6], (SCEN,), ((0, 8),), -0.2, 0.2)), 0.1, 1.0)
    scenario_node = different_ones(arg_keys[7], SCEN, G, 1, 0)
    return {"order_qty": order_qty, "multiplier": multiplier, "unit_cost": unit_cost, "demand": demand, "technology": technology, "kkt_inverse": kkt_inverse, "probability": probability, "scenario_node": scenario_node}


step_size = 0.5
penalty = 2.0


def reference(order_qty, multiplier, unit_cost, demand, technology, kkt_inverse, probability, scenario_node):
    supply = jnp.dot(technology.T, order_qty, preferred_element_type=jnp.float32)
    right_side = (demand.astype(jnp.float32) - supply).astype(jnp.bfloat16)
    recourse = jnp.dot(kkt_inverse, right_side, preferred_element_type=jnp.float32).astype(jnp.bfloat16)
    gradient = unit_cost.astype(jnp.float32) + multiplier + jnp.dot(technology, recourse, preferred_element_type=jnp.float32)
    planned = jnp.maximum(order_qty.astype(jnp.float32) - step_size * gradient, 0.0).astype(jnp.bfloat16)
    nodes = scenario_node[:, 0].astype(jnp.int32)
    weighted = planned.astype(jnp.float32) * probability[None, :]
    totals = jax.ops.segment_sum(weighted.T, nodes, num_segments=G).T
    masses = jax.ops.segment_sum(probability, nodes, num_segments=G)
    consensus = totals / masses[None, :]
    multiplier_next = multiplier + penalty * (planned.astype(jnp.float32) - consensus[:, nodes])
    return planned, recourse, consensus, multiplier_next
```

```python
import functools

import jax
import jax.numpy as jnp
from jax import lax
from jax.experimental import pallas as pl
from jax.experimental.pallas import tpu as pltpu
from jax.sharding import PartitionSpec as P

G = 512

step_size = 0.5
penalty = 2.0

bf16 = jnp.bfloat16
f32 = jnp.float32


CHUNKS = 4


def cost(flops, moved):
    return pl.CostEstimate(flops=int(flops), bytes_accessed=int(moved), transcendentals=0)


def swap(value, axis, size, bit):
    return lax.ppermute(value, axis, [(i, i ^ bit) for i in range(size)])


def full(shape):
    return pl.BlockSpec(shape, lambda *_: (0,) * len(shape))


def supply_blocks(technology, order_qty, ids, kinds, steps):
    depth, width = order_qty.shape
    count, parts = len(kinds), len(kinds[0])
    rows = technology.shape[1] // ids[1]
    part = width // parts
    tall = depth // steps

    def kernel(ids_ref, tech_ref, qty_ref, *rest):
        outs, total = rest[:-1], rest[-1]
        block, step = pl.program_id(0), pl.program_id(1)
        value = lax.dot_general(
            tech_ref[...], qty_ref[...], (((0,), (0,)), ((), ())), preferred_element_type=f32
        )

        @pl.when(step == 0)
        def _():
            total[...] = value

        @pl.when(step > 0)
        def _():
            total[...] += value

        for b in range(count):

            @pl.when((block == b) & (step == steps - 1))
            def _(b=b):
                for p in range(parts):
                    out = outs[b * parts + p]
                    out[...] = total[:, p * part : (p + 1) * part].astype(out.dtype)

    flat = [kind for block in kinds for kind in block]
    got = pl.pallas_call(
        kernel,
        grid_spec=pltpu.PrefetchScalarGridSpec(
            num_scalar_prefetch=1,
            grid=(count, steps),
            in_specs=[
                pl.BlockSpec((tall, rows), lambda b, k, ids: (k, ids[b])),
                pl.BlockSpec((tall, width), lambda b, k, ids: (k, 0)),
            ],
            out_specs=[full((rows, part))] * len(flat),
            scratch_shapes=[pltpu.VMEM((rows, width), f32)],
        ),
        out_shape=[jax.ShapeDtypeStruct((rows, part), kind) for kind in flat],
        cost_estimate=cost(
            2 * depth * width * rows * count, 2 * depth * (width + rows * count)
        ),
        name="supply",
    )(ids[0], technology, order_qty)
    return [got[b * parts : (b + 1) * parts] for b in range(count)]


def solve_part(kkt, pieces, ids, before, last):
    rows = kkt.shape[0]
    count, parts = len(pieces), len(pieces[0])
    tall, part = pieces[0][0].shape
    width = part * parts

    def kernel(ids_ref, kkt_ref, *rest):
        taken = rest[: count * parts]
        rest = rest[count * parts :]
        start = rest[0] if before is not None else None
        outs, total = rest[(before is not None) : -1], rest[-1]
        block = pl.program_id(0)

        @pl.when(block == 0)
        def _():
            total[...] = start[...] if before is not None else jnp.zeros_like(total)

        for b in range(count):

            @pl.when(block == b)
            def _(b=b):
                for p in range(parts):
                    total[:, p * part : (p + 1) * part] += jnp.dot(
                        kkt_ref[...], taken[b * parts + p][...], preferred_element_type=f32
                    )

        @pl.when(block == count - 1)
        def _():
            if last:
                outs[0][...] = total[...].astype(bf16)
                for p in range(parts):
                    outs[1 + p][...] = total[:, p * part : (p + 1) * part].astype(bf16)
            else:
                outs[0][...] = total[...]

    if last:
        shapes = [jax.ShapeDtypeStruct((rows, width), bf16)]
        shapes += [jax.ShapeDtypeStruct((rows, part), bf16)] * parts
    else:
        shapes = [jax.ShapeDtypeStruct((rows, width), f32)]
    operands = [piece for block in pieces for piece in block]
    operands += [before] if before is not None else []
    return pl.pallas_call(
        kernel,
        grid_spec=pltpu.PrefetchScalarGridSpec(
            num_scalar_prefetch=1,
            grid=(count,),
            in_specs=[pl.BlockSpec((rows, tall), lambda b, ids: (0, ids[b]))]
            + [full(o.shape) for o in operands],
            out_specs=[full(s.shape) for s in shapes],
            scratch_shapes=[pltpu.VMEM((rows, width), f32)],
        ),
        out_shape=shapes,
        cost_estimate=cost(
            2 * rows * width * tall * count, 2 * tall * count * (rows + width) + 8 * rows * width
        ),
        name="solve",
    )(ids, kkt, *operands)


def open_part(technology, pieces, ids, order_qty, multiplier, unit_cost, tiles):
    depth, width = order_qty.shape
    rows = depth // tiles
    parts = len(pieces)
    tall, part = pieces[0].shape

    def kernel(ids_ref, tech_ref, qty_ref, mult_ref, cost_ref, *rest):
        taken, out = rest[:-1], rest[-1]
        for p in range(parts):
            at = slice(p * part, (p + 1) * part)
            linked = jnp.dot(tech_ref[...], taken[p][...], preferred_element_type=f32)
            gradient = cost_ref[:, at].astype(f32) + mult_ref[:, at] + linked
            out[:, at] = qty_ref[:, at].astype(f32) - step_size * gradient

    row = pl.BlockSpec((rows, width), lambda i, ids: (i, 0))
    return pl.pallas_call(
        kernel,
        grid_spec=pltpu.PrefetchScalarGridSpec(
            num_scalar_prefetch=1,
            grid=(tiles,),
            in_specs=[pl.BlockSpec((rows, tall), lambda i, ids: (i, ids[0])), row, row, row]
            + [full((tall, part))] * parts,
            out_specs=row,
        ),
        out_shape=jax.ShapeDtypeStruct((depth, width), f32),
        cost_estimate=cost(2 * depth * width * tall, depth * (2 * tall + 12 * width)),
        name="open",
    )(ids, technology, order_qty, multiplier, unit_cost, *pieces)


def more_part(technology, pieces, ids, level, tiles):
    depth, width = level.shape
    rows = depth // tiles
    count, parts = len(pieces), len(pieces[0])
    tall, part = pieces[0][0].shape

    def kernel(ids_ref, *rest):
        tech, taken = rest[:count], rest[count : count + count * parts]
        level_ref, out = rest[-2:]
        for p in range(parts):
            at = slice(p * part, (p + 1) * part)
            linked = jnp.dot(tech[0][...], taken[p][...], preferred_element_type=f32)
            for b in range(1, count):
                linked += jnp.dot(
                    tech[b][...], taken[b * parts + p][...], preferred_element_type=f32
                )
            out[:, at] = level_ref[:, at] - step_size * linked

    row = pl.BlockSpec((rows, width), lambda i, ids: (i, 0))
    return pl.pallas_call(
        kernel,
        grid_spec=pltpu.PrefetchScalarGridSpec(
            num_scalar_prefetch=1,
            grid=(tiles,),
            in_specs=[
                pl.BlockSpec((rows, tall), lambda i, ids, b=b: (i, ids[b])) for b in range(count)
            ]
            + [full((tall, part))] * (count * parts)
            + [row],
            out_specs=row,
        ),
        out_shape=jax.ShapeDtypeStruct((depth, width), f32),
        input_output_aliases={1 + count + count * parts: 0},
        cost_estimate=cost(
            2 * depth * width * tall * count, depth * (2 * tall * count + 8 * width)
        ),
        name="more",
    )(ids, *([technology] * count), *[piece for block in pieces for piece in block], level)


def plan_chunk(technology, pieces, ids, level, weights, planned, chunk, chunks):
    depth, width = level.shape
    half = depth // chunks // 2
    parts = len(pieces)
    tall, part = pieces[0].shape
    nodes = weights.shape[1]

    def kernel(ids_ref, tech_ref, level_ref, weights_ref, *rest):
        taken = rest[:parts]
        plan_ref, away, own = rest[-3:]
        for p in range(parts):
            at = slice(p * part, (p + 1) * part)
            linked = jnp.dot(tech_ref[...], taken[p][...], preferred_element_type=f32)
            plan_ref[:, at] = jnp.maximum(level_ref[:, at] - step_size * linked, 0.0).astype(bf16)
        sums = jnp.dot(plan_ref[...], weights_ref[...], preferred_element_type=f32)

        @pl.when(pl.program_id(0) == 0)
        def _():
            away[...] = sums.astype(bf16)

        @pl.when(pl.program_id(0) == 1)
        def _():
            own[...] = sums

    def place(i, ids):
        return 2 * chunk + jnp.where(i == 0, 1 - ids[1], ids[1])

    row = pl.BlockSpec((half, width), lambda i, ids: (place(i, ids), 0))
    operands = [technology, level, weights, *pieces]
    in_specs = [
        pl.BlockSpec((half, tall), lambda i, ids: (place(i, ids), ids[0])),
        row,
        full(weights.shape),
    ] + [full((tall, part))] * parts
    aliases = {}
    if planned is not None:
        aliases = {1 + len(operands): 0}
        operands.append(planned)
        in_specs.append(pl.BlockSpec(memory_space=pl.ANY))
    return pl.pallas_call(
        kernel,
        grid_spec=pltpu.PrefetchScalarGridSpec(
            num_scalar_prefetch=1,
            grid=(2,),
            in_specs=in_specs,
            out_specs=[row, full((half, nodes)), full((half, nodes))],
        ),
        out_shape=[
            jax.ShapeDtypeStruct((depth, width), bf16),
            jax.ShapeDtypeStruct((half, nodes), bf16),
            jax.ShapeDtypeStruct((half, nodes), f32),
        ],
        input_output_aliases=aliases,
        cost_estimate=cost(
            4 * half * width * (tall + nodes), 2 * half * (2 * tall + 6 * width + 6 * nodes)
        ),
        name="plan",
    )(ids, *operands)


def close_chunk(own, away, member, multiplier, planned, ids, outs, chunk, chunks):
    depth, width = multiplier.shape
    half, nodes = own.shape

    def kernel(ids_ref, own_ref, away_ref, member_ref, mult_ref, plan_ref, *rest):
        cons_ref, next_ref = rest[-2:]

        def finish(source):
            sums = source[...]
            cons_ref[...] = sums.astype(f32)
            back = lax.dot_general(
                sums, member_ref[...], (((1,), (1,)), ((), ())), preferred_element_type=f32
            )
            next_ref[...] = mult_ref[...] + penalty * (plan_ref[...].astype(f32) - back)

        @pl.when(pl.program_id(0) == 0)
        def _():
            finish(own_ref)

        @pl.when(pl.program_id(0) == 1)
        def _():
            finish(away_ref)

    def place(i, ids):
        return 2 * chunk + jnp.where(i == 0, ids[0], 1 - ids[0])

    row = pl.BlockSpec((half, width), lambda i, ids: (place(i, ids), 0))
    node = pl.BlockSpec((half, nodes), lambda i, ids: (place(i, ids), 0))
    operands = [own, away, member, multiplier, planned]
    in_specs = [full(own.shape), full(away.shape), full(member.shape), row, row]
    aliases = {}
    if outs is not None:
        aliases = {1 + len(operands): 0, 2 + len(operands): 1}
        operands += outs
        in_specs += [pl.BlockSpec(memory_space=pl.ANY)] * 2
    return pl.pallas_call(
        kernel,
        grid_spec=pltpu.PrefetchScalarGridSpec(
            num_scalar_prefetch=1,
            grid=(2,),
            in_specs=in_specs,
            out_specs=[node, row],
        ),
        out_shape=[
            jax.ShapeDtypeStruct((depth, nodes), f32),
            jax.ShapeDtypeStruct((depth, width), f32),
        ],
        input_output_aliases=aliases,
        cost_estimate=cost(4 * half * width * nodes, 2 * half * (10 * width + 6 * nodes)),
        name="close",
    )(ids, *operands)


def line_sum(own, axis, size):
    length = size // 2
    spot = lax.axis_index(axis) // 2

    def both(pairs):
        return [(2 * a + c, 2 * b + c) for a, b in pairs for c in range(2)]

    total = own.astype(bf16)
    middle = length // 2
    for k in range(middle - 1):
        pairs = [(k, k + 1), (length - 1 - k, length - 2 - k)]
        came = lax.ppermute(total, axis, both(pairs))
        total = (total.astype(f32) + came.astype(f32)).astype(bf16)
    if length > 1:
        came = lax.ppermute(total, axis, both([(middle - 1, middle), (middle, middle - 1)]))
        total = (total.astype(f32) + came.astype(f32)).astype(bf16)
    for k in reversed(range(middle - 1)):
        pairs = [(k + 1, k), (length - 2 - k, length - 1 - k)]
        came = lax.ppermute(total, axis, both(pairs))
        total = jnp.where((spot == k) | (spot == length - 1 - k), came, total)
    return total


def on_device(
    n_dec,
    n_scen,
    order_qty,
    multiplier,
    unit_cost,
    demand,
    technology,
    kkt_inverse,
    probability,
    scenario_node,
):
    dec = lax.axis_index("dec").astype(jnp.int32)
    core = (lax.axis_index("scen") % 2).astype(jnp.int32)
    width = order_qty.shape[1]
    parts = 2
    part = width // parts
    bits = [1 << k for k in range(n_dec.bit_length() - 1)]
    orders = [bits, bits[::-1]]

    def ids_of(blocks):
        return dec ^ jnp.array(blocks, jnp.int32)

    member = scenario_node == jnp.arange(G, dtype=jnp.int32)[None, :]
    mass = jnp.sum(jnp.where(member, probability[:, None], 0.0), axis=0, keepdims=True)
    bit = 1
    while bit < n_scen:
        mass = mass + swap(mass, "scen", n_scen, bit)
        bit *= 2
    weights = jnp.where(member, probability[:, None] / mass, 0.0).astype(bf16)
    member = member.astype(bf16)

    groups = [g for g in ([n_dec - 1], list(range(1, n_dec - 1)), [0]) if g]
    held = {}
    for group in groups:
        kinds = [[bf16 if r & orders[p][0] else f32 for p in range(parts)] for r in group]
        got = supply_blocks(technology, order_qty, (ids_of(group), n_dec), kinds, 2)
        for r, pieces in zip(group, got):
            for p in range(parts):
                held[r, p] = pieces[p]
    right = []
    for p in range(parts):
        active = list(range(n_dec))
        for bit in orders[p]:
            for r in sorted((r for r in active if r & bit), reverse=True):
                came = swap(held[r, p].astype(bf16), "dec", n_dec, bit)
                held[r ^ bit, p] = held[r ^ bit, p] + came.astype(f32)
            active = [r for r in active if not r & bit]
        supply = held[0, p]
        at = slice(p * part, (p + 1) * part)
        right.append((demand[:, at].astype(f32) - supply).astype(bf16))

    def spread(own):
        have = {}
        for p in range(parts):
            have[0, p] = own[p]
            known = [0]
            for bit in reversed(orders[p]):
                for r in known:
                    have[r ^ bit, p] = swap(have[r, p], "dec", n_dec, bit)
                known = known + [r ^ bit for r in known]
        return [[have[r, p] for p in range(parts)] for r in range(n_dec)]

    rights = spread(right)
    early, late = list(range(n_dec - 1)), [n_dec - 1]
    (partial,) = solve_part(kkt_inverse, rights[:-1], ids_of(early), None, False)
    recourse, *own = solve_part(kkt_inverse, rights[-1:], ids_of(late), partial, True)

    solved = spread(own)
    level = open_part(
        technology, solved[0], ids_of([0]), order_qty, multiplier, unit_cost, 4
    )
    level = more_part(technology, solved[1:-1], ids_of(early[1:]), level, 4)
    last = jnp.stack([dec ^ (n_dec - 1), core])
    planned = None
    sums = []
    for chunk in range(CHUNKS):
        planned, away, keep = plan_chunk(
            technology, solved[-1], last, level, weights, planned, chunk, CHUNKS
        )
        sums.append((away, keep))
    outs = None
    for chunk in range(CHUNKS):
        away, keep = sums[chunk]
        keep = keep + swap(away, "scen", n_scen, 1).astype(f32)
        keep = line_sum(keep, "scen", n_scen)
        away = swap(keep, "scen", n_scen, 1)
        outs = close_chunk(
            keep, away, member, multiplier, planned, core[None], outs, chunk, CHUNKS
        )
    consensus, multiplier_next = outs
    return planned, recourse, consensus, multiplier_next


def solution(mesh):
    placed = (
        P("dec", "scen"),
        P("dec", "scen"),
        P("dec", "scen"),
        P("dec", "scen"),
        P("dec", None),
        P("dec", None),
        P("scen"),
        P("scen", None),
    )
    return jax.shard_map(
        functools.partial(on_device, mesh.shape["dec"], mesh.shape["scen"]),
        mesh=mesh,
        in_specs=placed,
        out_specs=(P("dec", "scen"), P("dec", "scen"), P("dec", None), P("dec", "scen")),
        check_vma=False,
    )
```
